256 devices in a mesh: fold: 4 (over x), trow: 32 (over z, y), tcol: 2 (over core).
Axes of the slice: x: 4, y: 4, z: 8, core: 2. Of those that a mesh axis runs over, the one named last changes fastest.
Arguments:
- samples: bfloat16 [8, 2048, 256], P('fold', ('trow', 'tcol')), may hold values from -6 to 6
- targets: bfloat16 [8, 2048, 128], P('fold', ('trow', 'tcol')), may hold values from -6 to 6
- frequencies: bfloat16 [256, 4096], replicated, may hold values from -1.5 to 1.5
- phases: float32 [4096], replicated, may hold values from -3.140625 to 3.140625
- valid_rows: int32 [8], P('fold'), may hold values from 1024 to 2048
- ridge: float32 [8], P('fold'), may hold values from 0.1 to 1
- low_bound: float32 [8], P('fold'), may hold values from 0.05 to 0.4
- high_bound: float32 [8], P('fold'), may hold values from 9 to 12
Outputs:
- iterate: float32 [8, 4096, 128], P('fold', 'tcol')
- residual: float32 [8, 4096, 128], P('fold', 'tcol')
The draws below stay inside these ranges and needn't reach their ends.
Inputs may be any that keep to these rules, and one draw needn't show every extreme that they name: Rows of fold k at positions valid_rows[k] and beyond take no part in any fit.
All inputs are finite; a program needn't handle non-finite values.
Results may differ from the reference program's by a relative error of at most 0.0046.
Values may be sent and summed in bfloat16 or wider, within the bound.
No kernel may reach another device: no remote copies, remote signals or barrier semaphores. Data moves between devices by JAX's collectives and lax.ppermute only.
A program may use at most 128 MiB of HBM per device.

```python
import math
import jax
import jax.numpy as jnp
from jax import lax

F = 4096
RAW = 256
TGT = 128
ROWS = 2048
ITERS = 2
FOLDS = 8


def with_ends(entries, rng, smallest, top_value):
    shape = entries.shape
    index_at = [jax.random.randint(jax.random.fold_in(rng, axis), (), 0, shape[axis]) for axis in range(len(shape))]
    entries = entries.at[tuple(index_at)].set(smallest)
    longest = shape.index(max(shape))
    index_at[longest] = (index_at[longest] + 1) % shape[longest]
    return entries.at[tuple(index_at)].set(top_value)


def levels(own_key, shape, split, low, top_value):
    loudness, own = 1.0, jax.random.fold_in(own_key, 6)
    for dim, blocks in split:
        steps = jnp.exp(jax.random.uniform(jax.random.fold_in(own, dim), (blocks,), jnp.float32, low / len(split), top_value / len(split)))
        loudness = loudness * jnp.repeat(steps, shape[dim] // blocks).reshape([-1 if axis == dim else 1 for axis in range(len(shape))])
    return loudness


def centred(rng, dims, scale, most, cuts=(), held_as=jnp.bfloat16):
    loudness = levels(rng, dims, cuts, -0.22, 0.18) if cuts else 1.0
    values = jax.random.normal(rng, dims, jnp.float32) * scale * loudness
    return jnp.minimum(jnp.maximum(values, -most), most).astype(held_as)


def setup_inputs(seed: int = 0) -> dict:
    key_of = jax.random.split(jax.random.key(seed), 9)
    return {
        "samples": centred(key_of[0], (FOLDS, ROWS, RAW), 1.0, 6.0, ((0, 4), (1, 64))),
        "targets": centred(key_of[1], (FOLDS, ROWS, TGT), 1.0, 6.0, ((0, 4), (1, 64))),
        "frequencies": centred(key_of[2], (RAW, F), (RAW // 16) ** -0.5, 1.5),
        "phases": jnp.clip(jax.random.uniform(key_of[3], (F,), jnp.float32, -3.140625, 3.140625), -3.140625, 3.140625),
        "valid_rows": with_ends(jax.random.randint(key_of[4], (FOLDS,), ROWS // 2, ROWS + 1), jax.random.fold_in(key_of[4], 1), ROWS // 2, ROWS).astype(jnp.int32),
        "ridge": jnp.clip(jnp.exp(math.log(1.0) - 2.3025851 * jax.random.uniform(key_of[5], (FOLDS,), jnp.float32) ** levels(key_of[5], (FOLDS,), ((0, 4),), -0.2, 0.2)), 0.1, 1.0),
        "low_bound": jnp.clip(0.05 + 0.35 * jax.random.uniform(key_of[6], (FOLDS,), jnp.float32) ** levels(key_of[6], (FOLDS,), ((0, 4),), -0.2, 0.2), 0.05, 0.4),
        "high_bound": jnp.clip(9.0 + 3.0 * jax.random.uniform(key_of[7], (FOLDS,), jnp.float32) ** levels(key_of[7], (FOLDS,), ((0, 4),), -0.2, 0.2), 9.0, 12.0),
    }


root_two = math.sqrt(2.0)

def reference(samples, targets, frequencies, phases, valid_rows, ridge, low_bound, high_bound):
    positions = jnp.arange(ROWS, dtype=jnp.int32)

    def advance(carry, item):
        gram_sum, cross_sum, count = carry
        sample_rows, target_rows, valid, shift, lower, upper = item
        angles = jnp.dot(sample_rows, frequencies, preferred_element_type=jnp.float32) + phases
        keep = (positions < valid).astype(jnp.float32)
        feats = (root_two * jnp.cos(angles) * keep[:, None]).astype(jnp.bfloat16)
        gram_sum = gram_sum + jnp.dot(feats.T, feats, preferred_element_type=jnp.float32)
        cross_sum = cross_sum + jnp.dot(feats.T, target_rows, preferred_element_type=jnp.float32)
        count = count + valid.astype(jnp.float32)
        matrix = gram_sum / count
        right_side = cross_sum / jnp.sqrt(count)
        center = (upper + lower) / 2.0 + shift
        spread = (upper - lower) / 2.0
        sigma = center / spread
        rho = 1.0 / sigma
        iterate = jnp.zeros_like(right_side)
        residual = right_side
        direction = right_side / center
        for turn in range(ITERS):
            iterate = iterate + direction
            image = jnp.dot(matrix, direction, precision=lax.Precision.HIGHEST) + shift * direction
            residual = residual - image
            rho_next = 1.0 / (2.0 * sigma - rho)
            direction = rho_next * rho * direction + 2.0 * rho_next / spread * residual
            rho = rho_next
        return ((gram_sum, cross_sum, count), (iterate, residual))
    start = (jnp.zeros((F, F), jnp.float32), jnp.zeros((F, TGT), jnp.float32), jnp.zeros((), jnp.float32))
    final, outputs = lax.scan(advance, start, (samples, targets, valid_rows, ridge, low_bound, high_bound))
    return (outputs[0], outputs[1])
```

```python
import functools
import math

import jax
import jax.numpy as jnp
import numpy as np
from jax import lax
from jax.experimental import pallas as pl
from jax.experimental.pallas import tpu as pltpu
from jax.sharding import Mesh, PartitionSpec as P

BF = jnp.bfloat16
F32 = jnp.float32
MARK = 1024.0
MAGIC = 12582912.0


def cosine_coefficients(degree=6):
    node = np.cos(np.pi * (np.arange(200) + 0.5) / 200)
    square = (node + 1.0) / 8.0
    fit = np.polynomial.Chebyshev.fit(
        square, math.sqrt(2.0) * np.cos(2 * np.pi * np.sqrt(square)), degree, domain=[0.0, 0.25]
    )
    return [float(v) for v in fit.convert(kind=np.polynomial.Polynomial).coef]


COS = cosine_coefficients()


def cosine_of_turns(turns):
    frac = turns - ((turns + MAGIC) - MAGIC)
    square = frac * frac
    total = jnp.full_like(square, COS[-1])
    for value in COS[-2::-1]:
        total = total * square + value
    return total


def gram_kernel(first, last, *refs):
    where_ref, *refs = refs
    xt_ref, wp_ref, wq_ref, pp_ref, pq_ref = refs[:5]
    if first:
        gacc, cacc = refs[5:]
    else:
        gin_ref, cin_ref, gacc, cacc = refs[5:]
    step = pl.program_id(0)

    @pl.when(step == 0)
    def _():
        if first:
            gacc[...] = jnp.zeros_like(gacc)
            cacc[...] = jnp.zeros_like(cacc)
        else:
            gacc[...] = gin_ref[...]
            cacc[...] = cin_ref[...]

    raw = wp_ref.shape[1]
    x = xt_ref[:, :raw]
    t = xt_ref[:, raw:]
    keep = jnp.where(x[:, 0:1].astype(F32) < MARK / 2, 1.0, 0.0)
    scale = 1.0 / (2 * math.pi)
    left = lax.dot_general(wp_ref[...], x, (((1,), (1,)), ((), ())), preferred_element_type=F32)
    left = cosine_of_turns(left * scale + pp_ref[...]).astype(BF)
    tile = 512
    for lo in range(0, wq_ref.shape[1], tile):
        cols = slice(lo, lo + tile)
        right = jnp.dot(x, wq_ref[:, cols], preferred_element_type=F32)
        right = (cosine_of_turns(right * scale + pq_ref[:, cols]) * keep).astype(BF)
        gacc[:, cols] += jnp.dot(left, right, preferred_element_type=F32)
        cacc[:, cols] += lax.dot_general(
            t, right, (((0,), (0,)), ((), ())), preferred_element_type=F32
        )
    if last:
        @pl.when(step == pl.num_programs(0) - 1)
        def _():
            z, y = where_ref[0], where_ref[1]
            count = where_ref[2].astype(F32)
            eye = lax.broadcasted_iota(jnp.int32, (64, 128), 0)
            lane = lax.broadcasted_iota(jnp.int32, (64, 128), 1) - lax.rem(z, 2) * 64
            eye = jnp.where(eye == lane, count, 0.0)
            for half in range(2):
                at = pl.multiple_of(half * 256 + y * 64, 64)
                lane_at = pl.multiple_of(half * 512 + lax.div(z, 2) * 128, 128)
                gacc[pl.ds(at, 64), pl.ds(lane_at, 128)] -= eye


def gram_call(spot, chunk, wp, wq, pp, pq, state, last):
    rows, step = chunk.shape[0], 256
    nl, nr, nt = wp.shape[0], wq.shape[1], chunk.shape[1] - wp.shape[1]
    whole = lambda a: pl.BlockSpec(a.shape, lambda i, s: (0,) * a.ndim)
    args = [chunk, wp, wq, pp, pq] + ([] if state is None else list(state))
    specs = [pl.BlockSpec((step, chunk.shape[1]), lambda i, s: (i, 0))] + [whole(a) for a in args[1:]]
    shapes = [(nl, nr), (nt, nr)]
    return pl.pallas_call(
        functools.partial(gram_kernel, state is None, last),
        grid_spec=pltpu.PrefetchScalarGridSpec(
            num_scalar_prefetch=1,
            grid=(rows // step,),
            in_specs=specs,
            out_specs=[pl.BlockSpec(s, lambda i, s: (0, 0)) for s in shapes],
        ),
        out_shape=[jax.ShapeDtypeStruct(s, F32) for s in shapes],
        compiler_params=pltpu.CompilerParams(vmem_limit_bytes=40 << 20),
        cost_estimate=pl.CostEstimate(
            flops=2 * rows * (nl * nr + wp.shape[1] * (nl + nr) + nt * nr),
            bytes_accessed=8 << 20,
            transcendentals=rows * (nl + nr),
        ),
        name="gram_rows",
    )(spot, *args)


def ring(n, s):
    return [(i, (i + s) % n) for i in range(n)]


def gather_z(blk):
    n = lax.axis_size("z")
    far = lax.ppermute(blk, "z", ring(n, n // 2))
    pair = jnp.concatenate([blk, far])
    up = lax.ppermute(pair, "z", ring(n, 1))
    down = lax.ppermute(pair, "z", ring(n, -1))
    two = lax.ppermute(pair, "z", ring(n, 2))
    return jnp.concatenate([pair, up, down, two])


Z_ORDER = (0, 4, 7, 3, 1, 5, 6, 2)


def gather_y(blk):
    n = lax.axis_size("y")
    half = blk.shape[0] // 2
    up = lax.ppermute(blk, "y", ring(n, 1))
    down = lax.ppermute(blk, "y", ring(n, -1))
    two_a = lax.ppermute(up[:half], "y", ring(n, 1))
    two_b = lax.ppermute(down[half:], "y", ring(n, -1))
    return blk, up, down, two_a, two_b


def place_kernel(where_ref, *refs):
    pieces, out_ref = refs[:-1], refs[-1]
    z, y = where_ref[0], where_ref[1]
    k, rows = out_ref.shape[0], 64
    blocks = [(p, i) for p in pieces for i in range(p.shape[0] // (k * rows))]
    offsets = [(dz, dy) for dy in (0, 3, 1, 2) for dz in Z_ORDER]
    for (piece, i), (dz, dy) in zip(blocks, offsets, strict=True):
        at = (lax.rem(y + dy, 4) * 8 + lax.rem(z + dz, 8)) * rows
        for q in range(k):
            out_ref[q, pl.ds(pl.multiple_of(at, rows), rows), :] = piece[
                (i * k + q) * rows : (i * k + q + 1) * rows, :
            ].astype(F32)


def place(pieces, z, y, k, features):
    cols = pieces[0].shape[1]
    return pl.pallas_call(
        place_kernel,
        grid_spec=pltpu.PrefetchScalarGridSpec(
            num_scalar_prefetch=1,
            grid=(),
            in_specs=[pl.BlockSpec(memory_space=pltpu.VMEM)] * len(pieces),
            out_specs=pl.BlockSpec(memory_space=pltpu.VMEM),
        ),
        out_shape=jax.ShapeDtypeStruct((k, features, cols), F32),
        name="place",
    )(jnp.stack([z, y]).astype(jnp.int32), *pieces)


def on_device(samples, targets, frequencies, phases, valid_rows, ridge, low_bound, high_bound):
    x, z, y, c = (lax.axis_index(a) for a in ("x", "z", "y", "c"))
    swap = [(0, 1), (1, 0)]
    pick = lambda a, i: lax.dynamic_index_in_dim(a, i, 0, False)
    rows = samples.shape[1]
    position = ((z * 4 + y) * 2 + c) * rows + lax.iota(jnp.int32, rows)
    keep = position[None, :] < valid_rows[:, None]
    both = jnp.concatenate(
        [jnp.where(keep[:, :, None], samples, jnp.asarray(MARK, BF)), targets], axis=2
    )
    mine = jnp.concatenate([pick(both, c), lax.ppermute(pick(both, 1 - c), "c", swap)])

    raw, width = frequencies.shape
    quarter = width // 8
    phases = (phases / (2 * math.pi)).reshape(1, width)
    cut = lambda a, at, size: lax.dynamic_slice_in_dim(a, at, size, 1)
    q_of = lambda a: jnp.concatenate([cut(a, (h * 4 + y) * quarter, quarter) for h in (0, 1)], 1)
    wq, pq = q_of(frequencies), q_of(phases)

    def p_of(a):
        wide = [cut(a, g * quarter + (z // 2) * 128, 128) for g in range(8)]
        tall = jnp.concatenate(wide, 1).T.reshape(8, 2, 64, a.shape[0])
        return lax.dynamic_index_in_dim(tall, z % 2, 1, False).reshape(width // 8, a.shape[0])

    wp, pp = p_of(frequencies), p_of(phases)
    spot = jnp.stack([z, y, pick(valid_rows, c)])

    blocks = gather_y(gather_z(mine))
    state = gram_call(spot, blocks[0], wp, wq, pp, pq, None, False)
    state = gram_call(spot, blocks[1], wp, wq, pp, pq, state, False)
    state = gram_call(spot, blocks[2], wp, wq, pp, pq, state, False)
    tail = jnp.concatenate(blocks[3:])
    gram, cross = gram_call(spot, tail, wp, wq, pp, pq, state, True)

    hp, hq = gram.shape[0] // 2, gram.shape[1] // 2
    halves = gram.reshape(2, hp, gram.shape[1])
    own = jnp.concatenate([pick(halves, c), cross])
    other = lax.ppermute(jnp.concatenate([pick(halves, 1 - c), cross]), "c", swap)
    even = jnp.where(c == 0, own, other)
    pair = own + other

    count = jnp.sum(valid_rows)
    digits = jnp.where(
        lax.broadcasted_iota(jnp.int32, (16, pair.shape[1]), 0) < 8, count // 64, count % 64
    )
    mine = cut(pair[hp:], c * hq, hq)
    high = mine.astype(BF)
    low = (mine - high.astype(F32)).astype(BF)
    load = jnp.concatenate(
        [pair[:hp].astype(BF), jnp.concatenate([high, low], 1), digits.astype(BF)]
    )
    edge = (load.shape[0] // 32) * 16
    up = lax.ppermute(load, "x", [(0, 1), (1, 2), (2, 3)])
    down = lax.ppermute(load, "x", [(0, 3), (1, 0)])
    up2 = lax.ppermute(up[:edge], "x", [(1, 2), (2, 3)])
    down2 = lax.ppermute(down[edge:], "x", [(3, 2), (0, 3)])
    before = up.astype(F32) + jnp.where(x == 3, down.astype(F32), 0.0)
    before = before + jnp.concatenate([up2, down2]).astype(F32)
    n_data = pair.shape[0]
    counted = before[n_data, 0] * 64.0 + before[n_data + 8, 0]
    n = counted + jnp.cumsum(valid_rows.astype(F32))
    half_cross = before[hp:n_data, :hq] + before[hp:n_data, hq:]
    rest_cross = lax.ppermute(half_cross, "c", swap)
    before_cross = jnp.where(
        c == 0,
        jnp.concatenate([half_cross, rest_cross], 1),
        jnp.concatenate([rest_cross, half_cross], 1),
    )

    tile = jnp.stack([before[:hp] + even[:hp], before[:hp] + pair[:hp]])
    right = jnp.stack([before_cross + even[hp:], before_cross + pair[hp:]])
    right = right / jnp.sqrt(n)[:, None, None]

    def dot(spec, a, b):
        return jnp.einsum(spec, a, b, precision=lax.Precision.HIGHEST)

    b = cut(right.reshape(-1, 2 * hq), c * hq + (z // 2) * 128, 128).reshape(2, -1, 128)
    b = lax.dynamic_slice_in_dim(jnp.swapaxes(b, 1, 2), (z % 2) * 64, 64, 1)

    part = dot("kpq,ktq->kpt", tile, right) / n[:, None, None]
    own_rows = lax.dynamic_slice_in_dim(part, y * 64, 64, 1) + b
    part = lax.dynamic_update_slice_in_dim(part, own_rows, y * 64, 1)
    sent = part.astype(BF)
    lost = (part - sent.astype(F32)).astype(BF)
    image, v = part, own_rows
    for s in (1, 3, 2):
        to = lax.rem(y + s, 4) * 64
        parcel = jnp.concatenate([sent, lax.dynamic_slice_in_dim(lost, to, 64, 1)], 1)
        parcel = lax.ppermute(parcel, "y", ring(4, s)).astype(F32)
        image = image + parcel[:, :hp]
        v = v + lax.dynamic_slice_in_dim(parcel, y * 64, 64, 1) + parcel[:, hp:]
    shift = ridge[:, None, None]
    center = ((high_bound + low_bound) / 2.0 + ridge)[:, None, None]
    spread = ((high_bound - low_bound) / 2.0)[:, None, None]
    sigma = center / spread
    rho = 1.0 / sigma
    rho_next = 1.0 / (2.0 * sigma - rho)
    keep_dir, add_res = rho_next * rho, 2.0 * rho_next / spread
    first = b / center
    res = b - (v / center + shift * first)
    second = keep_dir * first + add_res * res
    iterate = first + second
    out_blk = lambda a: a.astype(BF).reshape(-1, a.shape[2])
    features = width // 2
    out_iterate = place(gather_y(gather_z(out_blk(iterate))), z, y, 2, features)

    back = dot("kpq,kpt->kqt", tile, image) / n[:, None, None]
    back = back.reshape(2, 2, hq, back.shape[2])
    kept = lax.dynamic_index_in_dim(back, c, 1, False)
    given = lax.dynamic_index_in_dim(back, 1 - c, 1, False)
    kept = kept + lax.ppermute(given, "c", swap)
    kept = kept.astype(BF).reshape(2, 8, hq // 8, back.shape[3])
    w = v + jnp.sum(lax.all_to_all(kept, "z", 1, 1).astype(F32), axis=1)
    along = keep_dir / center * v + add_res * (v - w / center - shift / center * v)
    res = res - (along + shift * second)
    out_residual = place(gather_y(gather_z(out_blk(res))), z, y, 2, features)
    return out_iterate, out_residual


def solution(mesh):
    grid = Mesh(mesh.devices.reshape(4, 8, 4, 2), ("x", "z", "y", "c"))
    rows = P("x", ("z", "y", "c"), None)
    return jax.shard_map(
        on_device,
        mesh=grid,
        in_specs=(rows, rows, P(), P(), P("x"), P("x"), P("x"), P("x")),
        out_specs=(P("x", "c", None), P("x", "c", None)),
        check_vma=False,
    )
```

```python
import functools
import math

import jax
import jax.numpy as jnp
import numpy as np
from jax import lax
from jax.experimental import pallas as pl
from jax.experimental.pallas import tpu as pltpu
from jax.sharding import Mesh, PartitionSpec as P

BF = jnp.bfloat16
F32 = jnp.float32
SEND = jnp.float16
MARK = 1024.0
MAGIC = 12582912.0


def cosine_coefficients(degree=6):
    node = np.cos(np.pi * (np.arange(200) + 0.5) / 200)
    square = (node + 1.0) / 8.0
    fit = np.polynomial.Chebyshev.fit(
        square, math.sqrt(2.0) * np.cos(2 * np.pi * np.sqrt(square)), degree, domain=[0.0, 0.25]
    )
    return [float(v) for v in fit.convert(kind=np.polynomial.Polynomial).coef]


COS = cosine_coefficients()


def cosine_of_turns(turns):
    frac = turns - ((turns + MAGIC) - MAGIC)
    square = frac * frac
    total = jnp.full_like(square, COS[-1])
    for value in COS[-2::-1]:
        total = total * square + value
    return total


def gram_kernel(first, last, *refs):
    where_ref, *refs = refs
    xt_ref, wp_ref, wq_ref, pp_ref, pq_ref = refs[:5]
    if first:
        gacc, cacc = refs[5:]
    else:
        gin_ref, cin_ref, gacc, cacc = refs[5:]
    step = pl.program_id(0)

    @pl.when(step == 0)
    def _():
        if first:
            gacc[...] = jnp.zeros_like(gacc)
            cacc[...] = jnp.zeros_like(cacc)
        else:
            gacc[...] = gin_ref[...]
            cacc[...] = cin_ref[...]

    raw = wp_ref.shape[1]
    x = xt_ref[:, :raw]
    t = xt_ref[:, raw:]
    keep = jnp.where(x[:, 0:1].astype(F32) < MARK / 2, 1.0, 0.0)
    scale = 1.0 / (2 * math.pi)
    left = lax.dot_general(wp_ref[...], x, (((1,), (1,)), ((), ())), preferred_element_type=F32)
    left = cosine_of_turns(left * scale + pp_ref[...]).astype(BF)
    tile = 512
    for lo in range(0, wq_ref.shape[1], tile):
        cols = slice(lo, lo + tile)
        right = jnp.dot(x, wq_ref[:, cols], preferred_element_type=F32)
        right = (cosine_of_turns(right * scale + pq_ref[:, cols]) * keep).astype(BF)
        gacc[:, cols] += jnp.dot(left, right, preferred_element_type=F32)
        cacc[:, cols] += lax.dot_general(
            t, right, (((0,), (0,)), ((), ())), preferred_element_type=F32
        )
    if last:
        @pl.when(step == pl.num_programs(0) - 1)
        def _():
            z, y = where_ref[0], where_ref[1]
            count = where_ref[2].astype(F32)
            eye = lax.broadcasted_iota(jnp.int32, (64, 128), 0)
            lane = lax.broadcasted_iota(jnp.int32, (64, 128), 1) - lax.rem(z, 2) * 64
            eye = jnp.where(eye == lane, count, 0.0)
            for half in range(2):
                at = pl.multiple_of(half * 256 + y * 64, 64)
                lane_at = pl.multiple_of(half * 512 + lax.div(z, 2) * 128, 128)
                gacc[pl.ds(at, 64), pl.ds(lane_at, 128)] -= eye


def gram_call(spot, chunk, wp, wq, pp, pq, state, last):
    rows, step = chunk.shape[0], 256
    nl, nr, nt = wp.shape[0], wq.shape[1], chunk.shape[1] - wp.shape[1]
    whole = lambda a: pl.BlockSpec(a.shape, lambda i, s: (0,) * a.ndim)
    args = [chunk, wp, wq, pp, pq] + ([] if state is None else list(state))
    specs = [pl.BlockSpec((step, chunk.shape[1]), lambda i, s: (i, 0))] + [whole(a) for a in args[1:]]
    shapes = [(nl, nr), (nt, nr)]
    return pl.pallas_call(
        functools.partial(gram_kernel, state is None, last),
        grid_spec=pltpu.PrefetchScalarGridSpec(
            num_scalar_prefetch=1,
            grid=(rows // step,),
            in_specs=specs,
            out_specs=[pl.BlockSpec(s, lambda i, s: (0, 0)) for s in shapes],
        ),
        out_shape=[jax.ShapeDtypeStruct(s, F32) for s in shapes],
        compiler_params=pltpu.CompilerParams(vmem_limit_bytes=40 << 20),
        cost_estimate=pl.CostEstimate(
            flops=2 * rows * (nl * nr + wp.shape[1] * (nl + nr) + nt * nr),
            bytes_accessed=8 << 20,
            transcendentals=rows * (nl + nr),
        ),
        name="gram_rows",
    )(spot, *args)


def ring(n, s):
    return [(i, (i + s) % n) for i in range(n)]


def gather_z(blk):
    n = lax.axis_size("z")
    whole = lax.all_to_all(jnp.broadcast_to(blk[None], (n,) + blk.shape), "z", 0, 0)
    return jnp.swapaxes(whole, 0, 1).reshape(blk.shape[0], -1, blk.shape[2])


def gather_y(blk):
    n = lax.axis_size("y")
    half = blk.shape[0] // 2
    up = lax.ppermute(blk, "y", ring(n, 1))
    down = lax.ppermute(blk, "y", ring(n, -1))
    two_a = lax.ppermute(up[:half], "y", ring(n, 1))
    two_b = lax.ppermute(down[half:], "y", ring(n, -1))
    return blk, up, down, two_a, two_b


def spread_y(blk):
    n = lax.axis_size("y")
    y = lax.axis_index("y")
    k, rows, cols = blk.shape
    out = jnp.zeros((k, n * rows, cols), F32)
    zero = jnp.zeros((), jnp.int32)
    blk, up, down, two_a, two_b = gather_y(blk)
    for piece, lead, shift in ((blk, 0, 0), (up, 0, -1), (down, 0, 1), (two_a, 0, 2), (two_b, 1, 2)):
        at = lax.rem(y + n + shift, n) * rows
        out = lax.dynamic_update_slice(out, piece.astype(F32), (zero + lead, at, zero))
    return out


def reduce_y(part):
    n = lax.axis_size("y")
    parts = part.reshape(part.shape[0], n, -1, part.shape[2])
    return jnp.sum(lax.all_to_all(parts, "y", 1, 1), axis=1)


def on_device(samples, targets, frequencies, phases, valid_rows, ridge, low_bound, high_bound):
    x, z, y, c = (lax.axis_index(a) for a in ("x", "z", "y", "c"))
    swap = [(0, 1), (1, 0)]
    pick = lambda a, i: lax.dynamic_index_in_dim(a, i, 0, False)
    rows = samples.shape[1]
    position = ((z * 4 + y) * 2 + c) * rows + lax.iota(jnp.int32, rows)
    keep = position[None, :] < valid_rows[:, None]
    both = jnp.concatenate(
        [jnp.where(keep[:, :, None], samples, jnp.asarray(MARK, BF)), targets], axis=2
    )
    both = lax.all_to_all(jnp.tile(both, (8, 1, 1)), ("z", "c"), 0, 0)
    block = both.reshape(-1, both.shape[2])

    raw, width = frequencies.shape
    quarter = width // 8
    phases = (phases / (2 * math.pi)).reshape(1, width)
    cut = lambda a, at, size: lax.dynamic_slice_in_dim(a, at, size, 1)
    q_of = lambda a: jnp.concatenate([cut(a, (h * 4 + y) * quarter, quarter) for h in (0, 1)], 1)
    wq, pq = q_of(frequencies), q_of(phases)

    def p_of(a):
        wide = [cut(a, g * quarter + (z // 2) * 128, 128) for g in range(8)]
        tall = jnp.concatenate(wide, 1).T.reshape(8, 2, 64, a.shape[0])
        return lax.dynamic_index_in_dim(tall, z % 2, 1, False).reshape(width // 8, a.shape[0])

    wp, pp = p_of(frequencies), p_of(phases)
    spot = jnp.stack([z, y, pick(valid_rows, c)])

    blocks = gather_y(block)
    state = gram_call(spot, blocks[0], wp, wq, pp, pq, None, False)
    state = gram_call(spot, blocks[1], wp, wq, pp, pq, state, False)
    state = gram_call(spot, blocks[2], wp, wq, pp, pq, state, False)
    tail = jnp.concatenate(blocks[3:])
    gram, cross = gram_call(spot, tail, wp, wq, pp, pq, state, True)

    hp, hq = gram.shape[0] // 2, gram.shape[1] // 2
    halves = gram.reshape(2, hp, gram.shape[1])
    own = jnp.concatenate([pick(halves, c), cross])
    other = lax.ppermute(jnp.concatenate([pick(halves, 1 - c), cross]), "c", swap)
    even = jnp.where(c == 0, own, other)
    pair = own + other

    count = jnp.sum(valid_rows)
    digits = jnp.where(
        lax.broadcasted_iota(jnp.int32, (16, pair.shape[1]), 0) < 8, count // 64, count % 64
    )
    mine = cut(pair[hp:], c * hq, hq)
    nt = mine.shape[0]
    load = jnp.concatenate(
        [pair[:hp], jnp.concatenate([mine[: nt // 2], mine[nt // 2 :]], 1), digits.astype(F32)]
    ).astype(SEND)
    edge = (load.shape[0] // 32) * 16
    up = lax.ppermute(load, "x", [(0, 1), (1, 2), (2, 3)])
    down = lax.ppermute(load, "x", [(0, 3), (1, 0)])
    up2 = lax.ppermute(up[:edge], "x", [(1, 2), (2, 3)])
    down2 = lax.ppermute(down[edge:], "x", [(3, 2), (0, 3)])
    before = up.astype(F32) + jnp.where(x == 3, down.astype(F32), 0.0)
    before = before + jnp.concatenate([up2, down2]).astype(F32)
    n_data = hp + nt // 2
    counted = before[n_data, 0] * 64.0 + before[n_data + 8, 0]
    n = (counted + jnp.cumsum(valid_rows.astype(F32)))[:, None, None]
    half_cross = jnp.concatenate([before[hp:n_data, :hq], before[hp:n_data, hq:]])
    rest_cross = lax.ppermute(half_cross, "c", swap)
    before_cross = jnp.where(
        c == 0,
        jnp.concatenate([half_cross, rest_cross], 1),
        jnp.concatenate([rest_cross, half_cross], 1),
    )

    tile = jnp.stack([before[:hp] + even[:hp], before[:hp] + pair[:hp]])
    right = jnp.stack([before_cross + even[hp:], before_cross + pair[hp:]])
    right = right / jnp.sqrt(n)
    base = jnp.swapaxes(cut(right.reshape(-1, 2 * hq), c * hq, hq).reshape(2, nt, hq), 1, 2)
    b = lax.dynamic_slice_in_dim(base, z * 64, 64, 1)

    def apply(spec, a):
        return jnp.einsum(spec, tile, a, precision=lax.Precision.HIGHEST) / n

    v = b + reduce_y(apply("kpq,ktq->kpt", right))

    shift = ridge[:, None, None]
    center = ((high_bound + low_bound) / 2.0 + ridge)[:, None, None]
    spread = ((high_bound - low_bound) / 2.0)[:, None, None]
    sigma = center / spread
    rho = 1.0 / sigma
    rho_next = 1.0 / (2.0 * sigma - rho)
    keep_dir, add_res = rho_next * rho, 2.0 * rho_next / spread

    def step(b, v):
        first = b / center
        res = b - (v / center + shift * first)
        return first, res, keep_dir * first + add_res * res

    image = gather_z(v.astype(BF))
    first, _, second = step(base, image.astype(F32))
    out_iterate = spread_y((first + second).astype(BF))

    other = lax.ppermute(image, "c", swap)
    image = jnp.where(
        c == 0, jnp.concatenate([image, other], 1), jnp.concatenate([other, image], 1)
    )
    w = v + reduce_y(apply("kpq,kqt->kpt", image.astype(F32)))
    first, res, second = step(b, v)
    along = keep_dir / center * v + add_res * (v - w / center - shift / center * v)
    res = res - (along + shift * second)
    out_residual = spread_y(gather_z(res.astype(BF)))
    return out_iterate, out_residual


def solution(mesh):
    grid = Mesh(mesh.devices.reshape(4, 8, 4, 2), ("x", "z", "y", "c"))
    rows = P("x", ("z", "y", "c"), None)
    return jax.shard_map(
        on_device,
        mesh=grid,
        in_specs=(rows, rows, P(), P(), P("x"), P("x"), P("x"), P("x")),
        out_specs=(P("x", "c", None), P("x", "c", None)),
        check_vma=False,
    )
```
